32 devices in a mesh: dp: 8 (over z, x), mp: 4 (over y, core).
Axes of the slice: x: 2, y: 2, z: 4, core: 2. Of those that a mesh axis runs over, the one named last changes fastest.
Arguments:
- hidden_acts: bfloat16 [8192, 2048], P('dp', 'mp'), may hold values from -12 to 12
- out_cotangent: bfloat16 [8192, 1024], P('dp'), may hold values from -0.006629126 to 0.006629126
- left_stats: float32 [32, 512, 512], P('dp', 'mp'), may hold values from -0.35355339 to 5.3535534
- right_stats: float32 [32, 512, 512], P('dp', 'mp'), may hold values from -0.35355339 to 5.3535534
- left_roots: bfloat16 [32, 512, 512], P('dp', 'mp'), may hold values from -0.088388348 to 1.0883883
- right_roots: bfloat16 [32, 512, 512], P('dp', 'mp'), may hold values from -0.088388348 to 1.0883883
- owner_map: int32 [8], replicated, may hold values from 0 to 7, as said below
- owner_counts: int32 [8], replicated, may hold values from 0 to 4, as said below
Outputs:
- update: bfloat16 [8, 512, 512], P('dp', 'mp')
- new_left: float32 [32, 512, 512], P('dp', 'mp')
- new_right: float32 [32, 512, 512], P('dp', 'mp')
The draws below stay inside these ranges and needn't reach their ends.
Inputs may be any that keep to these rules, and one draw needn't show every extreme that they name: owner_map[b] is the dp index that keeps block b's statistics; index d owns exactly owner_counts[d] blocks, at most 4, and some index owns exactly 4 in every draw. owner_counts[d] is the number of blocks b with owner_map[b] = d; the counts sum to 8.
All inputs are finite; a program needn't handle non-finite values.
Results may differ from the reference program's by a relative error of at most 0.018.
Values may be sent and summed in bfloat16 or wider, within the bound.
No kernel may reach another device: no remote copies, remote signals or barrier semaphores. Data moves between devices by JAX's collectives and lax.ppermute only.
A program may use at most 64 MiB of HBM per device.

```python
import math
import jax
import jax.numpy as jnp
from jax import lax

BS = 512
NBC = 2
BPD = 1
TOK_DEV = 1024
CAP = 4
BLOCKS = 8
SLOTS = 32
NBR = 4
RB = 128
FW = 2048
DW = 1024
TOKENS = 8192
N_DP = 8
N_MP = 4


def column_scaled(key, rows, cols, factor):
    base_key, col_key = jax.random.split(key, 2)
    spread = jnp.exp(jax.random.uniform(col_key, (cols,), jnp.float32, math.log(0.3), math.log(3.0)))
    values = jnp.clip(jax.random.normal(base_key, (rows, cols), jnp.float32), -4.0, 4.0)
    return values * spread[None, :] * factor


def symmetric_slots(key, diagonal, spread):
    noise = jnp.clip(jax.random.normal(key, (SLOTS, BS, BS), jnp.float32), -4.0, 4.0)
    mixed = 0.5 * (noise + jnp.swapaxes(noise, 1, 2)) * (spread / math.sqrt(BS))
    return mixed + diagonal * jnp.eye(BS, dtype=jnp.float32)[None]


def owner_plan(key):
    base = jax.random.fold_in(key, 11)
    move_key, owner_key, block_key, flip_key = jax.random.split(base, 4)
    index_list = jnp.arange(N_DP, dtype=jnp.int32)
    counts = jnp.where(index_list == 0, 4 * BPD, jnp.where(index_list < 4, 0, BPD)).astype(jnp.int32)
    giver = (index_list >= 4) & ((index_list - 4) % 2 == 0) & (index_list + 1 < N_DP)
    moved = jnp.where(giver, jax.random.randint(move_key, (N_DP,), 0, BPD + 1, dtype=jnp.int32), 0).astype(jnp.int32)
    counts = counts - moved + jnp.roll(moved, 1)
    others = jnp.concatenate([jnp.arange(1, 5, dtype=jnp.int32), jnp.arange(6, N_DP, dtype=jnp.int32)])
    middle = (1 + jax.random.permutation(owner_key, N_DP - 2)).astype(jnp.int32)
    flip = jax.random.randint(flip_key, (), 0, 2, dtype=jnp.int32)
    first_end = (flip * (N_DP - 1)).astype(jnp.int32)
    second_end = ((1 - flip) * (N_DP - 1)).astype(jnp.int32)
    order = jnp.zeros((N_DP,), jnp.int32).at[others].set(middle).at[0].set(first_end).at[5].set(second_end)
    counts = jnp.zeros((N_DP,), jnp.int32).at[order].set(counts)
    ends = jnp.cumsum(counts).astype(jnp.int32)
    position = jnp.arange(BLOCKS, dtype=jnp.int32)
    sorted_owner = jnp.sum((ends[None, :] <= position[:, None]).astype(jnp.int32), axis=1)
    shuffle = jax.random.permutation(block_key, BLOCKS)
    assigned = sorted_owner[shuffle].astype(jnp.int32)
    first_owner = assigned[0]
    target = ((first_owner + 1) % N_DP).astype(jnp.int32)
    displaced = assigned[target]
    assigned = assigned.at[0].set(displaced).at[target].set(first_owner)
    return (assigned.astype(jnp.int32), counts.astype(jnp.int32))


def draw_hidden_acts(key, part):
    return column_scaled(jax.random.fold_in(key, 3), TOKENS, FW, 1.0).astype(jnp.bfloat16)


def draw_out_cotangent(key, part):
    return column_scaled(jax.random.fold_in(key, 5), TOKENS, DW, 0.05 / math.sqrt(TOKENS)).astype(jnp.bfloat16)


def draw_left_stats(key, part):
    return symmetric_slots(jax.random.fold_in(key, 7), 5.0, 2.0)


def draw_right_stats(key, part):
    return symmetric_slots(jax.random.fold_in(key, 13), 5.0, 2.0)


def draw_left_roots(key, part):
    return symmetric_slots(jax.random.fold_in(key, 17), 1.0, 0.5).astype(jnp.bfloat16)


def draw_right_roots(key, part):
    return symmetric_slots(jax.random.fold_in(key, 19), 1.0, 0.5).astype(jnp.bfloat16)


def draw_owner_map(key, part):
    return owner_plan(key)[0]


def draw_owner_counts(key, part):
    return owner_plan(key)[1]


def setup_inputs(seed: int = 0) -> dict:
    splits = jax.random.split(jax.random.key(seed), 9)
    hidden_acts = draw_hidden_acts(jax.random.fold_in(splits[8], 71), 0)
    out_cotangent = draw_out_cotangent(jax.random.fold_in(splits[8], 71), 0)
    left_stats = draw_left_stats(jax.random.fold_in(splits[8], 71), 0)
    right_stats = draw_right_stats(jax.random.fold_in(splits[8], 71), 0)
    left_roots = draw_left_roots(jax.random.fold_in(splits[8], 71), 0)
    right_roots = draw_right_roots(jax.random.fold_in(splits[8], 71), 0)
    owner_map = draw_owner_map(jax.random.fold_in(splits[8], 71), 0)
    owner_counts = draw_owner_counts(jax.random.fold_in(splits[8], 71), 0)
    return dict(hidden_acts=hidden_acts, out_cotangent=out_cotangent, left_stats=left_stats, right_stats=right_stats, left_roots=left_roots, right_roots=right_roots, owner_map=owner_map, owner_counts=owner_counts)


epsilon = 1e-06

def reference(hidden_acts, out_cotangent, left_stats, right_stats, left_roots, right_roots, owner_map, owner_counts):
    acts_split = hidden_acts.reshape(N_DP, TOK_DEV, FW)
    cotangents = out_cotangent.reshape(N_DP, TOK_DEV, DW)

    def accumulate(total_sum, act_pair):
        partial_value = lax.dot_general(act_pair[0], act_pair[1], (((0,), (0,)), ((), ())), preferred_element_type=jnp.float32)
        rounded = lax.optimization_barrier(partial_value.astype(jnp.bfloat16))
        return (total_sum + rounded.astype(jnp.float32), None)
    grad_sum, _ = lax.scan(accumulate, jnp.zeros((FW, DW), jnp.float32), (acts_split, cotangents))
    blocks = grad_sum.reshape(N_MP, NBR, RB, NBC, BS).transpose(1, 3, 0, 2, 4).reshape(BLOCKS, BS, BS)
    blocks = blocks.astype(jnp.bfloat16)
    block_ids = jnp.arange(BLOCKS, dtype=jnp.int32)
    same_owner = owner_map[:, None] == owner_map[None, :]
    owner_rank = lax.optimization_barrier(jnp.sum((same_owner & (block_ids[None, :] < block_ids[:, None])).astype(jnp.int32), axis=1)).astype(jnp.int32)
    is_live = (owner_rank < owner_counts[owner_map]) & (owner_rank < CAP)
    slot_of = jnp.where(is_live, owner_map * CAP + owner_rank, 0).astype(jnp.int32)

    def one_block(args):
        grad_block, where_slot, is_alive = args
        left_add = jnp.dot(grad_block, grad_block.T, preferred_element_type=jnp.float32)
        right_add = jnp.dot(grad_block.T, grad_block, preferred_element_type=jnp.float32)
        applied = jnp.dot(left_roots[where_slot], grad_block, preferred_element_type=jnp.float32).astype(jnp.bfloat16)
        conditioned = jnp.dot(applied, right_roots[where_slot], preferred_element_type=jnp.float32)
        widened = grad_block.astype(jnp.float32)
        scale_ratio = jnp.sqrt((jnp.mean(widened * widened) + epsilon) / (jnp.mean(conditioned * conditioned) + epsilon))
        keep_mask = is_alive.astype(jnp.float32)
        return (left_add * keep_mask, right_add * keep_mask, (conditioned * scale_ratio * keep_mask).astype(jnp.bfloat16))
    left_adds, right_adds, update = lax.map(one_block, (blocks, slot_of, is_live))
    slot_target = jnp.where(is_live, slot_of, SLOTS).astype(jnp.int32)
    new_left = left_stats.at[slot_target].add(left_adds, mode='drop')
    new_right = right_stats.at[slot_target].add(right_adds, mode='drop')
    return (update, new_left, new_right)
```

```python
import jax
import jax.numpy as jnp
from jax import lax
from jax.sharding import PartitionSpec as P

epsilon = 1e-06


def swap(value, axis, mask):
    size = lax.axis_size(axis)
    return lax.ppermute(value, axis, [(i, i ^ mask) for i in range(size)])


def narrow_sum(*terms):
    total = terms[0].astype(jnp.float32)
    for term in terms[1:]:
        total = total + term.astype(jnp.float32)
    return total.astype(jnp.bfloat16)


def at(stacked, index):
    return lax.dynamic_index_in_dim(stacked, index, 0, keepdims=False)


def lookup(table, index):
    ids = jnp.arange(table.shape[0], dtype=jnp.int32)
    return jnp.sum(jnp.where(ids == index, table, 0))


def reduce_to_home(hidden_acts, out_cotangent, myself, rows_piece, block_width):
    devices = lax.axis_size("dp")
    bands = devices // 2
    side = myself & 1
    band = myself >> 1
    dims = (((0,), (0,)), ((), ()))

    def half(which):
        columns = lax.dynamic_slice_in_dim(out_cotangent, which * block_width, block_width, 1)
        product = lax.dot_general(hidden_acts, columns, dims, preferred_element_type=jnp.float32)
        return product.astype(jnp.bfloat16).reshape(bands, rows_piece, block_width)

    away = half(1 - side)
    kept = half(side)
    order = list(range(bands - 1, -1, -1))
    received = {k: swap(at(away, band ^ k), "dp", 1) for k in order}
    pairs = {}
    for k in order:
        mine = lax.optimization_barrier(at(kept, band ^ k))
        pairs[k] = narrow_sum(received[k], mine)
    landed = [swap(pairs[k], "dp", 2 * k) for k in order if k]
    return narrow_sum(pairs[0], *landed)


def gather_dp(unit):
    devices = lax.axis_size("dp")
    units = {0: unit}
    masks = []
    step = devices // 2
    while step:
        masks.append(step)
        step //= 2
    for mask in masks:
        for key in sorted(units):
            units[key | mask] = swap(units[key], "dp", mask)
    return units


def gather_mp(unit):
    members = lax.axis_size("mp")
    units = {0: unit}
    for k in range(2, members, 2):
        units[k] = swap(unit, "mp", k)
    for k in range(0, members, 2):
        units[k + 1] = swap(units[k], "mp", 1)
    return units


def in_order(units, position):
    stacked = jnp.stack([units[k] for k in range(len(units))])
    return [at(stacked, position ^ k) for k in range(len(units))]


def route_home(roots, myself, owner_map, owner_rank):
    devices = lax.axis_size("dp")
    bits = devices.bit_length() - 1
    order = ([1, 0] + list(range(2, bits)))[:bits] if bits > 1 else [0]
    held = None
    fixed = 0
    for bit in order:
        mask = 1 << bit
        if held is None:
            other = swap(roots, "dp", mask)

            def packet(key, other=other, bit=bit):
                home = myself ^ key
                owner = lookup(owner_map, home)
                rank = lookup(owner_rank, home)
                mine = ((owner ^ myself) >> bit) & 1
                rank = jnp.clip(rank, 0, roots.shape[1] - 1)
                pick = lambda a: lax.dynamic_index_in_dim(a, rank, 1, keepdims=False)
                return jnp.where(mine == 0, pick(roots), pick(other))

            keys = [k for k in range(devices) if not k & mask]
            held = {k: packet(k) for k in keys}
        else:
            sent = [k for k in sorted(held) if k & mask]
            got = swap(jnp.stack([held[k] for k in sent]), "dp", mask)
            fresh = {}
            for place, k in enumerate(sent):
                key = k ^ mask
                owner = lookup(owner_map, myself ^ key)
                mine = ((owner ^ myself) >> bit) & 1
                fresh[key] = jnp.where(mine == 0, held[key], got[place])
            held = fresh
        fixed |= mask
    return held[0]


def shards(
    hidden_acts,
    out_cotangent,
    left_stats,
    right_stats,
    left_roots,
    right_roots,
    owner_map,
    owner_counts,
):
    devices = lax.axis_size("dp")
    myself = lax.axis_index("dp")
    column = lax.axis_index("mp")
    capacity, rows_piece, block_width = left_stats.shape
    blocks = owner_map.shape[0]
    block_ids = jnp.arange(blocks, dtype=jnp.int32)
    same_owner = owner_map[:, None] == owner_map[None, :]
    owner_rank = jnp.sum(
        (same_owner & (block_ids[None, :] < block_ids[:, None])).astype(jnp.int32), axis=1
    )
    owners = jnp.arange(devices, dtype=jnp.int32)
    held_count = jnp.sum(
        jnp.where(owner_map[:, None] == owners[None, :], owner_counts[None, :], 0), axis=1
    )
    is_live = (owner_rank < held_count) & (owner_rank < capacity)

    roots = route_home(jnp.stack([left_roots, right_roots]), myself, owner_map, owner_rank)
    grad = reduce_to_home(hidden_acts, out_cotangent, myself, rows_piece, block_width)
    everywhere = gather_dp(grad)
    stacked = jnp.stack([everywhere[k] for k in range(devices)])
    slots = []
    for s in range(capacity):
        match = (owner_map == myself) & is_live & (owner_rank == s)
        block = jnp.sum(jnp.where(match, block_ids, 0))
        slots.append(jnp.where(jnp.any(match), at(stacked, block ^ myself), jnp.zeros((), jnp.bfloat16)))
    own_rows = jnp.stack(slots)
    full_grad = jnp.concatenate(in_order(gather_mp(own_rows), column), axis=1)
    left_add = jnp.einsum("srk,stk->srt", own_rows, full_grad, preferred_element_type=jnp.float32)
    own_cols = lax.dynamic_slice_in_dim(full_grad, column * rows_piece, rows_piece, 2)
    right_add = jnp.einsum("skr,skt->srt", own_cols, full_grad, preferred_element_type=jnp.float32)
    new_left = left_stats + left_add
    new_right = right_stats + right_add

    home_grad = jnp.concatenate(in_order(gather_mp(grad), column), axis=0)
    full_roots = jnp.concatenate(in_order(gather_mp(roots), column), axis=1)
    applied = jnp.dot(full_roots[0], home_grad, preferred_element_type=jnp.float32).astype(jnp.bfloat16)
    conditioned = jnp.dot(applied, full_roots[1], preferred_element_type=jnp.float32)
    widened = home_grad.astype(jnp.float32)
    entries = float(block_width * block_width)
    grad_square = jnp.sum(widened * widened)
    cond_square = jnp.sum(conditioned * conditioned)
    ratio = jnp.sqrt((grad_square / entries + epsilon) / (cond_square / entries + epsilon))
    alive = jnp.any(is_live & (block_ids == myself))
    mine = lax.dynamic_slice_in_dim(conditioned, column * rows_piece, rows_piece, 0)
    update = jnp.where(alive, mine * ratio, 0.0).astype(jnp.bfloat16)[None]
    return (update, new_left, new_right)


def solution(mesh):
    in_specs = (
        P("dp", "mp"),
        P("dp", None),
        P("dp", "mp", None),
        P("dp", "mp", None),
        P("dp", "mp", None),
        P("dp", "mp", None),
        P(),
        P(),
    )
    out_specs = (P("dp", "mp", None), P("dp", "mp", None), P("dp", "mp", None))
    return jax.shard_map(shards, mesh=mesh, in_specs=in_specs, out_specs=out_specs, check_vma=False)
```
